32 devices in a mesh: exp: 8 (over z, y), slc: 4 (over x, core).
Axes of the slice: x: 2, y: 2, z: 4, core: 2. Of those that a mesh axis runs over, the one named last changes fastest.
Arguments:
- tokens: bfloat16 [16384, 1024], P(('exp', 'slc')), may hold values from -9 to 9
- ln1_gain: float32 [1024], replicated, may hold values from 0.5 to 1.5
- ln1_bias: float32 [1024], replicated, may hold values from -1 to 1
- qkv_weight: bfloat16 [3, 1024, 1024], P(None, None, 'slc'), may hold values from -0.1875 to 0.1875
- out_weight: bfloat16 [1024, 1024], P('slc'), may hold values from -0.75 to 0.75
- ln2_gain: float32 [1024], replicated, may hold values from 0.5 to 1.5
- ln2_bias: float32 [1024], replicated, may hold values from -1 to 1
- router_weight: bfloat16 [1024, 8], replicated, may hold values from -0.09375 to 0.09375
- up_weight: bfloat16 [1024, 4096], P(None, 'slc'), may hold values from -0.1875 to 0.1875
- down_weight: bfloat16 [4096, 1024], P('slc'), may hold values from -0.09375 to 0.09375
- expert_in: bfloat16 [8, 1024, 4096], P('exp', None, 'slc'), may hold values from -0.1875 to 0.1875
- expert_out: bfloat16 [8, 4096, 1024], P('exp', 'slc'), may hold values from -0.75 to 0.75
- mix: float32 [2], replicated, may hold values from 0.5 to 1.5
- expert_ids: int32 [16384, 1], P('exp'), may hold values from 0 to 7; in each aligned block of 512 rows (0 to 511, 512 to 1023, ...) at most 128 rows name the same one
- segment_ids: int32 [8, 2048], P('exp'), may hold values from 0 to 2, never falling along the last dimension, each value on 1 to 1024 neighbouring positions
- out_grad: bfloat16 [16384, 1024], P(('exp', 'slc')), may hold values from -6 to 6
Outputs:
- out: float32 [16384, 1024], P(('exp', 'slc'))
- grad_tokens: float32 [16384, 1024], P(('exp', 'slc'))
- grad_ln1_gain: float32 [1024], replicated
- grad_ln1_bias: float32 [1024], replicated
- grad_qkv_weight: float32 [3, 1024, 1024], P(None, 'exp', 'slc')
- grad_out_weight: float32 [1024, 1024], P('slc', 'exp')
- grad_ln2_gain: float32 [1024], replicated
- grad_ln2_bias: float32 [1024], replicated
- grad_router_weight: float32 [1024, 8], replicated
- grad_up_weight: float32 [1024, 4096], P('exp', 'slc')
- grad_down_weight: float32 [4096, 1024], P('slc', 'exp')
- grad_expert_in: float32 [8, 1024, 4096], P('exp', None, 'slc')
- grad_expert_out: float32 [8, 4096, 1024], P('exp', 'slc')
- grad_mix: float32 [2], replicated
- rms: float32 [4], replicated
The draws below stay inside these ranges and needn't reach their ends.
Inputs may be any that keep to these rules, and one draw needn't show every extreme that they name: `expert_ids`: in each aligned block of 512 rows (the rows of one device) no expert is named by more than 128 rows, a bound that some block reaches; every expert is named by some row. `segment_ids`: in each row the ids start at 0 and never fall; each of the 3 sequences spans 1 to 1024 positions, and one spans exactly 1024.
All inputs are finite; a program needn't handle non-finite values.
Results may differ from the reference program's by a relative error of at most 0.014.
Values may be sent and summed in bfloat16 or wider, within the bound.
No kernel may reach another device: no remote copies, remote signals or barrier semaphores. Data moves between devices by JAX's collectives and lax.ppermute only.
A program may use at most 256 MiB of HBM per device.

```python
import math
from functools import partial
import jax
import jax.numpy as jnp
import numpy as np
from jax import lax

D = 1024
HEADS = 16
HDIM = 64
FF = 4096
EFF = 4096
EXPERTS = 8
TOK_DEV = 512
SEGS = 3
GROUP = 2048
MAXLEN = 1024
CAP = 128
TOKENS = 16384
N_EXP = 8
N_SLC = 4


def draw_tokens(key, part):
    row_index = jnp.arange(TOKENS, dtype=jnp.float32)
    row_scale = 0.5 + row_index / TOKENS
    base_vals = jnp.clip(jax.random.normal(key, (TOKENS, D), jnp.float32), -6.0, 6.0)
    return (base_vals * row_scale[:, None]).astype(jnp.bfloat16)


def block_levels(own_key, extent, split, low, top_value):
    factor_of = 1.0
    for axis_at, parts in split:
        heights = jax.random.uniform(jax.random.fold_in(jax.random.fold_in(own_key, 6), axis_at), (parts,), jnp.float32, low / len(split), top_value / len(split))
        factor_of = factor_of * jnp.repeat(jnp.exp(heights), extent[axis_at] // parts).reshape((-1,) + (1,) * (len(extent) - 1 - axis_at))
    return factor_of


def length_profile(amount, total, limit, lean):
    weights = [(1 << 20) // math.isqrt(rank ** lean) + 1 for rank in range(2, amount + 1)]
    surplus, holding = total - limit - (amount - 1), [1] * (amount - 1)
    while surplus > 0:
        free = [i for i in range(amount - 1) if holding[i] < limit]
        mass, budget = sum([weights[i] for i in free]), surplus
        for i in free:
            addition = min(limit - holding[i], max(1, budget * weights[i] // mass), surplus)
            holding[i] = holding[i] + addition
            surplus = surplus - addition
    return np.array([limit] + holding)


def uneven_parts(rng, number_of, total, limit, lean):
    if number_of == 2:
        one = jax.random.randint(rng, (), max(1, total - limit), min(limit, total - 1) + 1)
        return jnp.stack([one, total - one])
    sizes = jnp.asarray(length_profile(number_of, total, limit, lean), jnp.int32)
    pairs = (number_of - 1) // 2
    donor, receiver = sizes[1:1 + 2 * pairs:2], sizes[2:2 + 2 * pairs:2]
    room = jnp.minimum(donor - 1, limit - receiver)
    passed = jax.random.randint(jax.random.fold_in(rng, 1), (pairs,), 0, 1 << 20) % (room + 1)
    sizes = sizes.at[1:1 + 2 * pairs:2].set(donor - passed).at[2:2 + 2 * pairs:2].set(receiver + passed)
    return sizes[jax.random.permutation(jax.random.fold_in(rng, 2), number_of)]


def routed_block(key, own, number, rows, count, top, limit, skew):
    ranking = jax.random.permutation(key, count)
    heavy_load, usual = portions_of(count, rows * top, limit, skew, True), portions_of(count, rows * top, limit, skew, False)
    places = jnp.arange(count)

    def named(lengths, offset_by):
        used = int((lengths > 0).sum())
        fixed = max(1, used // 4)
        shifted = fixed + (places - fixed + offset_by * (used - fixed)) % max(1, count - fixed)
        return jnp.zeros((count,), jnp.int32).at[ranking[jnp.where(places < fixed, places, shifted)]].set(jnp.asarray(lengths, jnp.int32))

    lengths = jnp.where(number % 4 == 0, named(heavy_load, number // 4), named(usual, number - number // 4 - 1))
    mixed = jax.random.permutation(jax.random.fold_in(own, 3), count)
    source_of, receiver = mixed[0:count // 2 * 2:2], mixed[1:count // 2 * 2:2]
    room = jnp.minimum(lengths[source_of] - 1, limit - lengths[receiver]) // 2
    room = jnp.where((source_of == ranking[0]) | (receiver == ranking[0]) | (lengths[receiver] == 0), 0, jnp.maximum(room, 0))
    shifted = jax.random.randint(jax.random.fold_in(own, 4), (count // 2,), 0, 1 << 20) % (room + 1)
    lengths = lengths.at[source_of].add(-shifted).at[receiver].add(shifted)
    items = jnp.searchsorted(jnp.cumsum(lengths), jnp.arange(rows * top), side="right").astype(jnp.int32)
    grid = items.reshape(top, rows).T
    grid = grid[jax.random.permutation(jax.random.fold_in(own, 1), rows)]
    offset_by = jax.random.randint(jax.random.fold_in(own, 2), (rows, 1), 0, top)
    return jnp.take_along_axis(grid, (jnp.arange(top)[None, :] + offset_by) % top, axis=1)


def portions_of(count, total, bound, slope, full):
    weights = [(1 << 20) // math.isqrt(rank ** slope) + 1 for rank in range(1, count + 1)]
    largest = bound if full else min(bound, max(-(-total // count), total * weights[0] // sum(weights)))
    least = 1 if total - largest >= count - 1 else 0
    given, spare = [largest] + [least] * (count - 1), total - largest - least * (count - 1)
    while spare > 0:
        candidates = [i for i in range(1, count) if given[i] < largest] or [i for i in range(1, count) if given[i] < bound]
        whole, remaining = sum([weights[i] for i in candidates]), spare
        for i in candidates:
            extra = min(bound - given[i], max(1, remaining * weights[i] // whole), spare)
            given[i] = given[i] + extra
            spare = spare - extra
    return np.array(given)


def noise(stream_key, shape, width, reach, cuts=(), kind=jnp.bfloat16):
    values = jax.random.normal(stream_key, shape, jnp.float32) * width
    if len(cuts) > 0:
        values = block_levels(stream_key, shape, cuts, -0.22, 0.18) * values
    return jnp.clip(values, min=-reach, max=reach).astype(kind)


def setup_inputs(seed: int = 0) -> dict:
    arg_keys = jax.random.split(jax.random.key(seed), 17)
    tokens = draw_tokens(jax.random.fold_in(arg_keys[16], 71), 0)
    ln1_gain = jnp.clip(1.0 + 0.1 * jax.random.normal(arg_keys[1], (D,), jnp.float32), 0.5, 1.5)
    ln1_bias = noise(arg_keys[2], (D,), 0.2, 1.0, (), jnp.float32)
    qkv_weight = noise(arg_keys[3], (3, D, D), D ** -0.5, 0.1875, ((2, 4),))
    out_weight = noise(arg_keys[4], (D, D), (D // 16) ** -0.5, 0.75, ((0, 4),))
    ln2_gain = jnp.clip(1.0 + 0.1 * jax.random.normal(arg_keys[5], (D,), jnp.float32), 0.5, 1.5)
    ln2_bias = noise(arg_keys[6], (D,), 0.2, 1.0, (), jnp.float32)
    router_weight = noise(arg_keys[7], (D, EXPERTS), (4 * D) ** -0.5, 0.09375)
    up_weight = noise(arg_keys[8], (D, FF), D ** -0.5, 0.1875, ((1, 4),))
    down_weight = noise(arg_keys[9], (FF, D), FF ** -0.5, 0.09375, ((0, 4),))
    expert_in = noise(arg_keys[10], (EXPERTS, D, EFF), D ** -0.5, 0.1875, ((0, 8), (2, 4)))
    expert_out = noise(arg_keys[11], (EXPERTS, EFF, D), (max(1, EFF // (EXPERTS * EXPERTS))) ** -0.5, 0.75, ((0, 8), (1, 4)))
    mix = jnp.clip(jax.random.uniform(arg_keys[12], (2,), jnp.float32, 0.5, 1.5), 0.5, 1.5)
    expert_ids_keys = jax.random.split(jax.random.fold_in(arg_keys[13], 1), TOKENS // TOK_DEV)
    expert_ids_turns = jax.random.permutation(jax.random.fold_in(arg_keys[13], 3), TOKENS // TOK_DEV)
    expert_ids = jax.vmap(lambda own, number: routed_block(jax.random.fold_in(arg_keys[13], 2), own, number, TOK_DEV, EXPERTS, 1, CAP, 2))(expert_ids_keys, expert_ids_turns).reshape((TOKENS, 1))
    segment_ids = jax.vmap(lambda own: jnp.searchsorted(jnp.cumsum(uneven_parts(own, SEGS, GROUP, MAXLEN, 2)), jnp.arange(GROUP), side="right"))(jax.random.split(arg_keys[14], N_EXP)).reshape((N_EXP, GROUP)).astype(jnp.int32)
    out_grad = noise(arg_keys[15], (TOKENS, D), 1.0, 6.0, ((0, 32),))
    return {"tokens": tokens, "ln1_gain": ln1_gain, "ln1_bias": ln1_bias, "qkv_weight": qkv_weight, "out_weight": out_weight, "ln2_gain": ln2_gain, "ln2_bias": ln2_bias, "router_weight": router_weight, "up_weight": up_weight, "down_weight": down_weight, "expert_in": expert_in, "expert_out": expert_out, "mix": mix, "expert_ids": expert_ids, "segment_ids": segment_ids, "out_grad": out_grad}


@jax.custom_vjp
def low(v):
    return lax.optimization_barrier(v.astype(jnp.bfloat16)).astype(jnp.float32)

@jax.custom_vjp
def low_back(v):
    return v

def low_keep(v):
    return (low(v), None)

def low_pass(kept, grad):
    return (grad,)

def back_keep(v):
    return (v, None)

def back_low(kept, grad):
    return (low(grad),)
low.defvjp(low_keep, low_pass)
low_back.defvjp(back_keep, back_low)
EPSILON = 1e-05
NEG_BIG = -1e+30
PRECISE = lax.Precision.HIGHEST

def layer_norm(values, gain_vec, shift_vec):
    row_mean = lax.optimization_barrier(jnp.mean(values, axis=-1, keepdims=True))
    centered = values - row_mean
    variance = lax.optimization_barrier(jnp.mean(centered * centered, axis=-1, keepdims=True))
    return centered * lax.rsqrt(variance + EPSILON) * gain_vec + shift_vec

def root_mean(values):
    return jnp.sqrt(jnp.mean(values * values))

def attend_group(item_pair):
    qkv_group, seg_ids = item_pair
    queries = qkv_group[:, 0]
    keys_all = qkv_group[:, 1]
    values_all = qkv_group[:, 2]
    scores = jnp.einsum('qhd,khd->hqk', queries, keys_all, precision=PRECISE) * HDIM ** (-0.5)
    scores = low_back(scores)
    positions = jnp.arange(GROUP, dtype=jnp.int32)
    allowed = (seg_ids[:, None] == seg_ids[None, :]) & (positions[None, :] <= positions[:, None])
    scores = jnp.where(allowed[None], scores, NEG_BIG)
    prob_rows = low(jax.nn.softmax(scores, axis=-1))
    return jnp.einsum('hqk,khd->qhd', prob_rows, values_all, precision=PRECISE)

def run_expert(item_triple):
    expert_rows, first_weight, second_weight = item_triple
    pre_act = low_back(jnp.dot(expert_rows, first_weight, precision=PRECISE))
    act_low = low(jax.nn.gelu(pre_act))
    return jnp.dot(act_low, second_weight, precision=PRECISE)

def forward(ids_flat, seg_all, x_in, gain_one, bias_one, w_qkv, w_out, gain_two, bias_two, w_router, w_up, w_down, w_first, w_second, mix_pair):
    xn1 = low(layer_norm(x_in, gain_one, bias_one))
    qkv = low_back(low(jnp.einsum('td,kdc->tkc', xn1, w_qkv, precision=PRECISE)))
    shaped = qkv.reshape(N_EXP, GROUP, 3, HEADS, HDIM)
    attn_o = lax.map(jax.checkpoint(attend_group), (shaped, seg_all))
    attn_o = low_back(low(attn_o.reshape(TOKENS, D)))
    attn = low_back(jnp.dot(attn_o, w_out, precision=PRECISE))
    h_res = x_in + attn
    xn2 = low(layer_norm(h_res, gain_two, bias_two))
    hot_mask = ids_flat[:, None] == jnp.arange(EXPERTS, dtype=jnp.int32)[None, :]
    logits = low_back(jnp.dot(xn2, w_router, precision=PRECISE))
    prob_router = jax.nn.softmax(logits, axis=-1)
    gate_value = lax.optimization_barrier(jnp.sum(jnp.where(hot_mask, prob_router, 0.0), axis=-1))
    up_pre = low_back(jnp.dot(xn2, w_up, precision=PRECISE))
    dense = jnp.dot(low(jax.nn.gelu(up_pre)), w_down, precision=PRECISE)
    expert_x = low_back(xn2)
    hot_int = hot_mask.astype(jnp.int32).reshape(N_EXP * N_SLC, TOK_DEV, EXPERTS)
    before = jnp.cumsum(hot_int, axis=1) - hot_int
    slot_rank = lax.optimization_barrier(jnp.sum(before * hot_int, axis=-1)).reshape(TOKENS)
    column = jnp.arange(TOKENS, dtype=jnp.int32) // TOK_DEV * CAP + slot_rank
    buffer = jnp.zeros((EXPERTS, N_EXP * N_SLC * CAP, D), expert_x.dtype).at[ids_flat, column].set(expert_x)
    expert_res = lax.map(jax.checkpoint(run_expert), (buffer, w_first, w_second))
    expert_res = low_back(low(expert_res))
    expert_tok = expert_res[ids_flat, column]
    mixed_out = mix_pair[0] * dense + (mix_pair[1] * gate_value)[:, None] * expert_tok
    y_out = h_res + mixed_out
    root_means = jnp.stack([root_mean(h_res), root_mean(attn), root_mean(mixed_out), root_mean(y_out)])
    return (y_out, root_means)

def reference(tokens, ln1_gain, ln1_bias, qkv_weight, out_weight, ln2_gain, ln2_bias, router_weight, up_weight, down_weight, expert_in, expert_out, mix, expert_ids, segment_ids, out_grad):
    float_args = (tokens.astype(jnp.float32), ln1_gain, ln1_bias, qkv_weight.astype(jnp.float32), out_weight.astype(jnp.float32), ln2_gain, ln2_bias, router_weight.astype(jnp.float32), up_weight.astype(jnp.float32), down_weight.astype(jnp.float32), expert_in.astype(jnp.float32), expert_out.astype(jnp.float32), mix)
    y_out, pull_back, root_means = jax.vjp(partial(forward, expert_ids[:, 0], segment_ids), *float_args, has_aux=True)
    gradients = pull_back(out_grad.astype(jnp.float32))
    return (y_out, gradients[0], gradients[1], gradients[2], gradients[3], gradients[4], gradients[5], gradients[6], gradients[7], gradients[8], gradients[9], gradients[10], gradients[11], gradients[12], root_means)
```

```python
import functools

import jax
import jax.numpy as jnp
from jax import lax
from jax.experimental import pallas as pl
from jax.experimental.pallas import tpu as pltpu
from jax.sharding import PartitionSpec as P

HDIM = 64
EPSILON = 1e-05
NEG_BIG = -1e30
TILE = 256
BF16 = jnp.bfloat16
F32 = jnp.float32


def norm_rows(values, gain_vec, shift_vec):
    row_mean = jnp.mean(values, axis=-1, keepdims=True)
    centered = values - row_mean
    inv_std = lax.rsqrt(jnp.mean(centered * centered, axis=-1, keepdims=True) + EPSILON)
    normed = centered * inv_std
    return (normed * gain_vec + shift_vec, normed, inv_std)


def norm_back(grad_in, normed, inv_std, gain_vec):
    scaled = grad_in * gain_vec
    combined = (
        scaled
        - jnp.mean(scaled, -1, keepdims=True)
        - normed * jnp.mean(scaled * normed, -1, keepdims=True)
    )
    return (combined * inv_std, jnp.sum(grad_in * normed, 0), jnp.sum(grad_in, 0))


def gelu_back(pre_act, grad_act):
    return jax.vjp(jax.nn.gelu, pre_act)[1](grad_act)[0]


def dot(a, b, dims, out=F32):
    return lax.dot_general(a, b, (dims, ((), ())), preferred_element_type=out)


NN = ((1,), (0,))
NT = ((1,), (1,))
TN = ((0,), (0,))


def after(value, *deps):
    return lax.optimization_barrier((value, *deps))[0]


def swap(value, axis, bits):
    size = lax.axis_size(axis)
    return lax.ppermute(value, axis, [(a, a ^ bits) for a in range(size)])


def gather_rel(value, axis):
    size = lax.axis_size(axis)
    have = {0: value}
    bit = size // 2
    while bit:
        have.update({r | bit: swap(v, axis, bit) for r, v in list(have.items())})
        bit //= 2
    return [have[r] for r in range(size)]


def scatter_rel(parts, axis):
    size = lax.axis_size(axis)
    have = dict(enumerate(parts))
    bit = 1
    while bit < size:
        have = {
            r: v + swap(have[r | bit].astype(BF16), axis, bit).astype(F32)
            for r, v in have.items()
            if not r & bit
        }
        bit *= 2
    return have[0]


def exchange_rel(parts, axis):
    return [parts[0]] + [swap(parts[r], axis, r) for r in range(1, len(parts))]


def exchange_slots(slots, axis):
    size = lax.axis_size(axis)
    if size <= 8:
        return jnp.concatenate(exchange_rel([slots[r] for r in range(size)], axis), 0)
    order = jnp.arange(size, dtype=jnp.int32) ^ lax.axis_index(axis)
    moved = lax.all_to_all(jnp.take(slots, order, axis=0), axis, 0, 0, tiled=True)
    return jnp.take(moved, order, axis=0).reshape(-1, slots.shape[-1])


def scatter_rows(value, axis):
    size = lax.axis_size(axis)
    index = lax.axis_index(axis)
    rows, cols = value.shape
    cur = value.reshape(size, rows // size, cols)
    bit = 1
    while bit < size:
        pair = cur.reshape(cur.shape[0] // 2, 2, rows // size, cols)
        mine = (index // bit) % 2
        keep = lax.dynamic_index_in_dim(pair, mine, 1, keepdims=False)
        give = lax.dynamic_index_in_dim(pair, 1 - mine, 1, keepdims=False)
        cur = keep + swap(give.astype(BF16), axis, bit).astype(F32)
        bit *= 2
    return cur[0]


def sum_all(value, axes):
    for axis in axes:
        bit = 1
        while bit < lax.axis_size(axis):
            value = value + swap(value, axis, bit)
            bit *= 2
    return value


def row_offset(block, own, rows_own):
    per = rows_own // TILE
    return pl.multiple_of(((block // per) ^ own) * rows_own + (block % per) * TILE, TILE)


def attn_fwd_kernel(rows_own, info, qkv, qstart, o_ref, lse_ref, vt_ref, acc_ref):
    group_rows, width = o_ref.shape
    heads = width // HDIM
    own = info[0]
    vt_ref[...] = qkv[:, 2 * width :].T
    lane_head = lax.broadcasted_iota(jnp.int32, (TILE, width), 1) // HDIM
    k_iota = lax.broadcasted_iota(jnp.int32, (TILE, TILE), 0)
    q_iota = lax.broadcasted_iota(jnp.int32, (TILE, TILE), 1)

    def q_block(i, _):
        row = row_offset(i, own, rows_own)
        q = qkv[pl.ds(row, TILE), :width] * jnp.asarray(HDIM**-0.5, BF16)
        qh = [jnp.where(lane_head == h, q, jnp.zeros_like(q)) for h in range(heads)]
        first = qstart[:, pl.ds(pl.multiple_of(i * TILE, TILE), TILE)]

        def step(j, stats, diag):
            at = row_offset(j, own, rows_own)
            k = qkv[pl.ds(at, TILE), width : 2 * width]
            allowed = k_iota >= first - j * TILE
            if diag:
                allowed = allowed & (k_iota <= q_iota)
            out = []
            for h in range(heads):
                s = jnp.where(allowed, dot(k, qh[h], NT), NEG_BIG)
                top = jnp.max(s, 0, keepdims=True)
                if not diag:
                    old_top, old_sum = stats[h]
                    top = jnp.maximum(top, old_top)
                    fade = jnp.exp(old_top - top)
                p = jnp.exp(s - top)
                total = jnp.sum(p, 0, keepdims=True)
                rows = slice(h * HDIM, (h + 1) * HDIM)
                pv = dot(vt_ref[rows, pl.ds(at, TILE)], p.astype(BF16), NN)
                if not diag:
                    total = total + old_sum * fade
                    pv = pv + acc_ref[rows] * fade
                acc_ref[rows] = pv
                out.append((top, total))
            return tuple(out)

        stats = step(i, None, True)
        stats = lax.fori_loop(info[1 + i], i, lambda j, c: step(j, c, False), stats)
        for h in range(heads):
            rows = slice(h * HDIM, (h + 1) * HDIM)
            acc_ref[rows] = acc_ref[rows] * (1.0 / stats[h][1])
        o_ref[pl.ds(row, TILE), :] = acc_ref[...].T.astype(BF16)
        lse = jnp.concatenate([top + jnp.log(total) for top, total in stats], 0)
        lse_ref[:, pl.ds(pl.multiple_of(i * TILE, TILE), TILE)] = lse
        return 0

    lax.fori_loop(0, group_rows // TILE, q_block, 0)


def attn_bwd_kernel(
    rows_own, info, qkv, qstart, o_ref, do_ref, lse_ref, out_ref, kt_ref, dk_ref, dv_ref, dq_ref
):
    group_rows, width = o_ref.shape
    heads = width // HDIM
    own = info[0]
    kt_ref[...] = qkv[:, width : 2 * width].T
    dk_ref[...] = jnp.zeros_like(dk_ref)
    dv_ref[...] = jnp.zeros_like(dv_ref)
    lane_head = lax.broadcasted_iota(jnp.int32, (TILE, width), 1) // HDIM
    k_iota = lax.broadcasted_iota(jnp.int32, (TILE, TILE), 0)
    q_iota = lax.broadcasted_iota(jnp.int32, (TILE, TILE), 1)
    pick = (
        lax.broadcasted_iota(jnp.int32, (8, width), 1) // HDIM
        == lax.broadcasted_iota(jnp.int32, (8, width), 0)
    ).astype(F32)

    def q_block(i, _):
        row = row_offset(i, own, rows_own)
        cols = pl.ds(pl.multiple_of(i * TILE, TILE), TILE)
        q = qkv[pl.ds(row, TILE), :width] * jnp.asarray(HDIM**-0.5, BF16)
        do = do_ref[pl.ds(row, TILE), :]
        none = jnp.zeros_like(q)
        qh = [jnp.where(lane_head == h, q, none) for h in range(heads)]
        doh = [jnp.where(lane_head == h, do, none) for h in range(heads)]
        first = qstart[:, cols]
        lse = lse_ref[:, cols]
        delta = lax.dot_general(
            pick,
            do.astype(F32) * o_ref[pl.ds(row, TILE), :].astype(F32),
            (NT, ((), ())),
            precision=lax.Precision.HIGHEST,
            preferred_element_type=F32,
        )
        dq_ref[...] = jnp.zeros_like(dq_ref)

        def step(j, diag):
            at = row_offset(j, own, rows_own)
            k = qkv[pl.ds(at, TILE), width : 2 * width]
            v = qkv[pl.ds(at, TILE), 2 * width :]
            allowed = k_iota >= first - j * TILE
            if diag:
                allowed = allowed & (k_iota <= q_iota)
            dk = jnp.zeros((TILE, width), F32)
            dv = jnp.zeros((TILE, width), F32)
            for h in range(heads):
                s = jnp.where(allowed, dot(k, qh[h], NT), NEG_BIG)
                p = jnp.exp(s - lse[h : h + 1])
                ds = (p * (dot(v, doh[h], NT) - delta[h : h + 1])).astype(BF16)
                dv = dv + dot(p.astype(BF16), doh[h], NN)
                dk = dk + dot(ds, qh[h], NN)
                rows = slice(h * HDIM, (h + 1) * HDIM)
                dq_ref[rows] += dot(kt_ref[rows, pl.ds(at, TILE)], ds, NN)
            dk_ref[pl.ds(at, TILE), :] += dk
            dv_ref[pl.ds(at, TILE), :] += dv

        step(i, True)

        def body(j, _):
            step(j, False)
            return 0

        lax.fori_loop(info[1 + i], i, body, 0)
        out_ref[pl.ds(row, TILE), :width] = (dq_ref[...].T * HDIM**-0.5).astype(BF16)
        return 0

    lax.fori_loop(0, group_rows // TILE, q_block, 0)
    out_ref[:, width : 2 * width] = dk_ref[...].astype(BF16)
    out_ref[:, 2 * width :] = dv_ref[...].astype(BF16)


def attn_call(kernel, rows_own, info, operands, outs, scratch, name):
    smem = pl.BlockSpec(memory_space=pltpu.SMEM)
    vmem = pl.BlockSpec(memory_space=pltpu.VMEM)
    return pl.pallas_call(
        functools.partial(kernel, rows_own),
        out_shape=outs,
        in_specs=[smem] + [vmem] * len(operands),
        out_specs=[vmem] * len(outs),
        scratch_shapes=scratch,
        name=name,
    )(info, *operands)


def local(
    tokens,
    ln1_gain,
    ln1_bias,
    qkv_weight,
    out_weight,
    ln2_gain,
    ln2_bias,
    router_weight,
    up_weight,
    down_weight,
    expert_in,
    expert_out,
    mix,
    expert_ids,
    segment_ids,
    out_grad,
):
    slices = lax.axis_size("slc")
    slc_index = lax.axis_index("slc")
    exp_index = lax.axis_index("exp")
    rows_own, features = tokens.shape
    group_rows = rows_own * slices
    experts = router_weight.shape[1]
    capacity = max(2, 2 * rows_own // experts)
    slots = experts * capacity
    width = qkv_weight.shape[2]
    heads = width // HDIM
    mix_dense = mix[0]
    mix_expert = mix[1]

    ids_own = lax.dynamic_slice_in_dim(expert_ids[:, 0], slc_index * rows_own, rows_own, 0)
    rel_ids = ids_own ^ exp_index
    hot = (rel_ids[:, None] == jnp.arange(experts, dtype=jnp.int32)[None]).astype(BF16)
    token_iota = jnp.arange(rows_own, dtype=jnp.int32)
    earlier = (token_iota[None] < token_iota[:, None]).astype(BF16)
    rank = jnp.sum(dot(earlier, hot, NN) * hot.astype(F32), -1).astype(jnp.int32)
    slot_own = rel_ids * capacity + rank
    select = (jnp.arange(slots, dtype=jnp.int32)[:, None] == slot_own[None]).astype(BF16)

    def to_experts(rows):
        packed = dot(select, rows, NN, BF16).reshape(experts, capacity, features)
        return exchange_slots(packed, "exp")

    def from_experts(rows):
        home = exchange_slots(rows.reshape(experts, capacity, features), "exp")
        return dot(select, home, TN)

    x_own = tokens.astype(F32)
    xn1, hat_one, inv_one = norm_rows(x_own, ln1_gain, ln1_bias)
    xg_one = jnp.concatenate(gather_rel(xn1.astype(BF16), "slc"), 0)
    qkv_flat = jnp.transpose(qkv_weight, (1, 0, 2)).reshape(features, 3 * width)
    qkv = dot(xg_one, qkv_flat, NN, BF16)
    seg = segment_ids[0]
    qstart = jnp.sum((seg[None] < seg[:, None]).astype(jnp.int32), -1)
    info = jnp.concatenate([slc_index[None].astype(jnp.int32), qstart[::TILE] // TILE])
    qstart = qstart[None]
    attn_o, lse = attn_call(
        attn_fwd_kernel,
        rows_own,
        info,
        (qkv, qstart),
        [
            jax.ShapeDtypeStruct((group_rows, width), BF16),
            jax.ShapeDtypeStruct((heads, group_rows), F32),
        ],
        [pltpu.VMEM((width, group_rows), BF16), pltpu.VMEM((width, TILE), F32)],
        "attn_fwd",
    )

    grad_y_low = after(out_grad, xg_one)
    grad_slots = to_experts(grad_y_low)
    wo_all = jnp.concatenate(gather_rel(after(out_weight, xg_one), "slc"), 0)
    win = gather_rel(after(expert_in[0], xg_one), "slc")
    wout = gather_rel(after(expert_out[0], xg_one), "slc")
    grad_group = jnp.concatenate(gather_rel(grad_y_low, "slc"), 0)

    def blocks(value):
        return [value[r * rows_own : (r + 1) * rows_own] for r in range(slices)]

    o_own = jnp.concatenate(exchange_rel(blocks(attn_o), "slc"), 1)
    attn_own = dot(o_own, wo_all, NN)
    h_own = x_own + attn_own
    xn2, hat_two, inv_two = norm_rows(h_own, ln2_gain, ln2_bias)
    xn2_low = xn2.astype(BF16)

    rows_in = to_experts(xn2_low)
    xg_two = jnp.concatenate(gather_rel(xn2_low, "slc"), 0)
    up_pre = dot(xg_two, up_weight, NN)
    hidden = jax.nn.gelu(up_pre).astype(BF16)
    dense_own = scatter_rel(blocks(dot(hidden, down_weight, NN)), "slc")
    grad_hidden = mix_dense * dot(grad_group, down_weight, NT)
    grad_up_pre = gelu_back(up_pre, grad_hidden).astype(BF16)
    dense_back = scatter_rel(blocks(dot(grad_up_pre, up_weight, NT)), "slc")
    grad_up = dot(xg_two, grad_up_pre, TN)
    grad_down_t = mix_dense * dot(grad_group, hidden, TN)

    prob_router = jax.nn.softmax(dot(rows_in, router_weight, NN), axis=-1)
    hot_here = (jnp.arange(experts, dtype=jnp.int32) == exp_index).astype(F32)[None]
    gate = jnp.sum(prob_router * hot_here, -1, keepdims=True)
    grad_rows = grad_slots.astype(F32)
    grad_eo = (mix_expert * gate * grad_rows).astype(BF16)
    pre, act = [], []
    eo = None
    for r in range(slices):
        a = dot(rows_in, win[r], NN)
        z = jax.nn.gelu(a).astype(BF16)
        part = dot(z, wout[r], NN)
        eo = part if eo is None else eo + part
        pre.append(a.astype(BF16))
        act.append(z)
    eo_low = eo.astype(BF16).astype(F32)
    gated = gate * eo_low
    row_dot = jnp.sum(grad_rows * eo_low, -1, keepdims=True)
    grad_gate = mix_expert * row_dot
    grad_logits = (gate * (hot_here - prob_router) * grad_gate).astype(BF16)
    grad_router = dot(rows_in, grad_logits, TN)
    back = dot(grad_logits, router_weight, NT)
    gin, gout = [], []
    for r in range(slices):
        gz = dot(grad_eo, wout[r], NT)
        ga = gelu_back(pre[r].astype(F32), gz).astype(BF16)
        back = back + dot(ga, win[r], NT)
        gin.append(dot(rows_in, ga, TN))
        gout.append(dot(act[r], grad_eo, TN))
    back_low = back.astype(BF16)
    expert_back = from_experts(back_low)
    gated_own = from_experts(after(gated.astype(BF16), expert_back))
    grad_ein = scatter_rel(gin, "slc")
    grad_eout = scatter_rel(gout, "slc")

    mixed_out = mix_dense * dense_own + mix_expert * gated_own
    y_own = h_own + mixed_out
    grad_y = out_grad.astype(F32)

    grad_xn2 = dense_back + expert_back
    grad_h_norm, grad_gain_two, grad_bias_two = norm_back(grad_xn2, hat_two, inv_two, ln2_gain)
    grad_h = grad_y + grad_h_norm
    grad_attn = grad_h.astype(BF16)

    grad_o_own = dot(grad_attn, wo_all, NT, BF16)
    grad_o = jnp.concatenate(
        exchange_rel([grad_o_own[:, r * width : (r + 1) * width] for r in range(slices)], "slc"), 0
    )
    grad_wo_t = dot(grad_attn, o_own, TN)
    grad_wo_t = scatter_rel(
        [grad_wo_t[:, r * width : (r + 1) * width] for r in range(slices)], "slc"
    )
    (grad_qkv,) = attn_call(
        attn_bwd_kernel,
        rows_own,
        info,
        (qkv, qstart, attn_o, grad_o, lse),
        [jax.ShapeDtypeStruct((group_rows, 3 * width), BF16)],
        [
            pltpu.VMEM((width, group_rows), BF16),
            pltpu.VMEM((group_rows, width), F32),
            pltpu.VMEM((group_rows, width), F32),
            pltpu.VMEM((width, TILE), F32),
        ],
        "attn_bwd",
    )
    grad_xn1 = scatter_rel(blocks(dot(grad_qkv, qkv_flat, NT)), "slc")
    grad_qkv_w = dot(xg_one, grad_qkv, TN)
    grad_x_norm, grad_gain_one, grad_bias_one = norm_back(grad_xn1, hat_one, inv_one, ln1_gain)
    grad_x = grad_h + grad_x_norm

    sum_up = scatter_rows(grad_up, "exp")
    sum_down = scatter_rows(grad_down_t, "exp").T
    sum_wo = scatter_rows(grad_wo_t, "exp").T
    sum_qkv = scatter_rows(grad_qkv_w, "exp")
    sum_qkv = jnp.transpose(sum_qkv.reshape(-1, 3, width), (1, 0, 2))

    scalars = jnp.stack(
        [
            jnp.sum(h_own * h_own),
            jnp.sum(attn_own * attn_own),
            jnp.sum(mixed_out * mixed_out),
            jnp.sum(y_own * y_own),
            jnp.sum(grad_y * dense_own),
            jnp.sum(gate * row_dot),
        ]
    )
    early = jnp.concatenate(
        [
            grad_gain_two,
            grad_bias_two,
            grad_router.reshape(-1),
            jnp.pad(scalars, (0, features - scalars.shape[0])),
        ]
    ).reshape(-1, 128)
    early = sum_all(early, ("slc", "exp")).reshape(-1)
    late = jnp.concatenate([grad_gain_one, grad_bias_one]).reshape(-1, 128)
    late = sum_all(late, ("slc", "exp")).reshape(-1)
    router_end = (2 + experts) * features
    scalars = early[router_end : router_end + 6]
    entry_total = group_rows * lax.axis_size("exp") * features
    return (
        y_own,
        grad_x,
        late[:features],
        late[features:],
        sum_qkv,
        sum_wo,
        early[:features],
        early[features : 2 * features],
        early[2 * features : router_end].reshape(features, experts),
        sum_up,
        sum_down,
        grad_ein[None],
        grad_eout[None],
        scalars[4:6],
        jnp.sqrt(scalars[:4] / entry_total),
    )


def solution(mesh):
    in_specs = (
        P(("exp", "slc"), None),
        P(),
        P(),
        P(None, None, "slc"),
        P("slc", None),
        P(),
        P(),
        P(),
        P(None, "slc"),
        P("slc", None),
        P("exp", None, "slc"),
        P("exp", "slc", None),
        P(),
        P("exp", None),
        P("exp", None),
        P(("exp", "slc"), None),
    )
    out_specs = (
        P(("exp", "slc"), None),
        P(("exp", "slc"), None),
        P(),
        P(),
        P(None, "exp", "slc"),
        P("slc", "exp"),
        P(),
        P(),
        P(),
        P("exp", "slc"),
        P("slc", "exp"),
        P("exp", None, "slc"),
        P("exp", "slc", None),
        P(),
        P(),
    )
    return jax.shard_map(local, mesh=mesh, in_specs=in_specs, out_specs=out_specs, check_vma=False)
```

```python
import functools

import jax
import jax.numpy as jnp
from jax import lax
from jax.experimental import pallas as pl
from jax.experimental.pallas import tpu as pltpu
from jax.sharding import PartitionSpec as P


HDIM = 64
EPSILON = 1e-05
NEG_BIG = -1e30
TILE = 256
BF16 = jnp.bfloat16
F32 = jnp.float32


def dot(a, b, dims, out=F32):
    return lax.dot_general(a, b, (dims, ((), ())), preferred_element_type=out)


SLC = "slc"
EXP = "exp"


NN = ((1,), (0,))
NT = ((1,), (1,))
TN = ((0,), (0,))


def norm_rows(values, gain_vec, shift_vec):
    row_mean = jnp.mean(values, axis=-1, keepdims=True)
    centered = values - row_mean
    inv_std = lax.rsqrt(jnp.mean(centered * centered, axis=-1, keepdims=True) + EPSILON)
    normed = centered * inv_std
    return (normed * gain_vec + shift_vec, normed, inv_std)


def norm_back(grad_in, normed, inv_std, gain_vec):
    scaled = grad_in * gain_vec
    combined = (
        scaled
        - jnp.mean(scaled, -1, keepdims=True)
        - normed * jnp.mean(scaled * normed, -1, keepdims=True)
    )
    return (combined * inv_std, jnp.sum(grad_in * normed, 0), jnp.sum(grad_in, 0))


def gelu_pair(pre_act):
    v = pre_act.astype(F32)
    root = 0.7978845608028654
    t = jnp.tanh(root * (v + 0.044715 * v * v * v))
    slope = 0.5 * (1.0 + t) + (0.5 * root) * v * (1.0 - t * t) * (1.0 + 0.134145 * v * v)
    return ((0.5 * v * (1.0 + t)).astype(BF16), slope.astype(BF16))


def after(value, *deps):
    return lax.optimization_barrier((value, *deps))[0]


def swap(value, axis, bits):
    size = lax.axis_size(axis)
    return lax.ppermute(value, axis, [(a, a ^ bits) for a in range(size)])


def gather_rel(value, axis):
    size = lax.axis_size(axis)
    have = {0: value}
    bit = size // 2
    while bit:
        have.update({r | bit: swap(v, axis, bit) for r, v in list(have.items())})
        bit //= 2
    return [have[r] for r in range(size)]


def scatter_rel(parts, axis, holds=()):
    size = lax.axis_size(axis)
    have = dict(enumerate(parts))
    bit = 1
    while bit < size:
        if holds and bit == size // 2:
            chunks = jnp.split(have[bit].astype(BF16), len(holds))
            moved = []
            for n, chunk in enumerate(chunks):
                moved.append(swap(holds[n](chunk), axis, bit))
            return lax.optimization_barrier(have[0]) + jnp.concatenate(moved, 0).astype(F32)
        have = {
            r: v.astype(F32) + swap(have[r | bit].astype(BF16), axis, bit).astype(F32)
            for r, v in have.items()
            if not r & bit
        }
        bit *= 2
    return have[0]


def exchange_rel(parts, axis):
    return [parts[0]] + [swap(parts[r], axis, r) for r in range(1, len(parts))]


def scatter_rows(values, axis):
    size = lax.axis_size(axis)
    index = lax.axis_index(axis)
    rows = values[0].shape[0] // size
    curs = [v.reshape(size, rows, v.shape[1]) for v in values]
    bit = 1
    while bit < size:
        pairs = [c.reshape(c.shape[0] // 2, 2, rows, c.shape[2]) for c in curs]
        mine = (index // bit) % 2
        keep = [lax.dynamic_index_in_dim(p, mine, 1, keepdims=False) for p in pairs]
        give = [lax.dynamic_index_in_dim(p, 1 - mine, 1, keepdims=False) for p in pairs]
        got = swap(jnp.concatenate([g.astype(BF16) for g in give], 2), axis, bit)
        at = 0
        curs = []
        for k in keep:
            curs.append(k + got[..., at : at + k.shape[2]].astype(F32))
            at += k.shape[2]
        bit *= 2
    return [c[0] for c in curs]


def sum_all(value, axes):
    for axis in axes:
        bit = 1
        while bit < lax.axis_size(axis):
            value = value + swap(value, axis, bit)
            bit *= 2
    return value


def row_offset(block, own, rows_own):
    per = rows_own // TILE
    return pl.multiple_of(((block // per) ^ own) * rows_own + (block % per) * TILE, TILE)


def attn_fwd_kernel(rows_own, info, qkv, qstart, o_ref, lse_ref, vt_ref, acc_ref):
    group_rows, width = o_ref.shape
    heads = width // HDIM
    own = info[0]
    vt_ref[...] = qkv[:, 2 * width :].T
    lane_head = lax.broadcasted_iota(jnp.int32, (TILE, width), 1) // HDIM
    k_iota = lax.broadcasted_iota(jnp.int32, (TILE, TILE), 0)
    q_iota = lax.broadcasted_iota(jnp.int32, (TILE, TILE), 1)

    def q_block(i, _):
        row = row_offset(i, own, rows_own)
        q = qkv[pl.ds(row, TILE), :width] * jnp.asarray(HDIM**-0.5, BF16)
        qh = [jnp.where(lane_head == h, q, jnp.zeros_like(q)) for h in range(heads)]
        first = qstart[:, pl.ds(pl.multiple_of(i * TILE, TILE), TILE)]

        def step(j, stats, diag):
            at = row_offset(j, own, rows_own)
            k = qkv[pl.ds(at, TILE), width : 2 * width]
            allowed = k_iota >= first - j * TILE
            if diag:
                allowed = allowed & (k_iota <= q_iota)
            out = []
            for h in range(heads):
                s = jnp.where(allowed, dot(k, qh[h], NT), NEG_BIG)
                top = jnp.max(s, 0, keepdims=True)
                if not diag:
                    old_top, old_sum = stats[h]
                    top = jnp.maximum(top, old_top)
                    fade = jnp.exp(old_top - top)
                p = jnp.exp(s - top)
                total = jnp.sum(p, 0, keepdims=True)
                rows = slice(h * HDIM, (h + 1) * HDIM)
                pv = dot(vt_ref[rows, pl.ds(at, TILE)], p.astype(BF16), NN)
                if not diag:
                    total = total + old_sum * fade
                    pv = pv + acc_ref[rows] * fade
                acc_ref[rows] = pv
                out.append((top, total))
            return tuple(out)

        stats = step(i, None, True)
        stats = lax.fori_loop(info[1 + i], i, lambda j, c: step(j, c, False), stats)
        for h in range(heads):
            rows = slice(h * HDIM, (h + 1) * HDIM)
            acc_ref[rows] = acc_ref[rows] * (1.0 / stats[h][1])
        o_ref[pl.ds(row, TILE), :] = acc_ref[...].T.astype(BF16)
        lse = jnp.concatenate([top + jnp.log(total) for top, total in stats], 0)
        lse_ref[:, pl.ds(pl.multiple_of(i * TILE, TILE), TILE)] = lse
        return 0

    lax.fori_loop(0, group_rows // TILE, q_block, 0)


def attn_bwd_kernel(
    rows_own, info, qkv, qstart, o_ref, do_ref, lse_ref, out_ref, kt_ref, dk_ref, dv_ref, dq_ref
):
    group_rows, width = o_ref.shape
    heads = width // HDIM
    own = info[0]
    kt_ref[...] = qkv[:, width : 2 * width].T
    dk_ref[...] = jnp.zeros_like(dk_ref)
    dv_ref[...] = jnp.zeros_like(dv_ref)
    lane_head = lax.broadcasted_iota(jnp.int32, (TILE, width), 1) // HDIM
    k_iota = lax.broadcasted_iota(jnp.int32, (TILE, TILE), 0)
    q_iota = lax.broadcasted_iota(jnp.int32, (TILE, TILE), 1)
    pick = (
        lax.broadcasted_iota(jnp.int32, (8, width), 1) // HDIM
        == lax.broadcasted_iota(jnp.int32, (8, width), 0)
    ).astype(F32)

    def q_block(i, _):
        row = row_offset(i, own, rows_own)
        cols = pl.ds(pl.multiple_of(i * TILE, TILE), TILE)
        q = qkv[pl.ds(row, TILE), :width] * jnp.asarray(HDIM**-0.5, BF16)
        do = do_ref[pl.ds(row, TILE), :]
        none = jnp.zeros_like(q)
        qh = [jnp.where(lane_head == h, q, none) for h in range(heads)]
        doh = [jnp.where(lane_head == h, do, none) for h in range(heads)]
        first = qstart[:, cols]
        lse = lse_ref[:, cols]
        delta = lax.dot_general(
            pick,
            do.astype(F32) * o_ref[pl.ds(row, TILE), :].astype(F32),
            (NT, ((), ())),
            precision=lax.Precision.HIGHEST,
            preferred_element_type=F32,
        )
        dq_ref[...] = jnp.zeros_like(dq_ref)

        def step(j, diag):
            at = row_offset(j, own, rows_own)
            k = qkv[pl.ds(at, TILE), width : 2 * width]
            v = qkv[pl.ds(at, TILE), 2 * width :]
            allowed = k_iota >= first - j * TILE
            if diag:
                allowed = allowed & (k_iota <= q_iota)
            dk = jnp.zeros((TILE, width), F32)
            dv = jnp.zeros((TILE, width), F32)
            for h in range(heads):
                s = jnp.where(allowed, dot(k, qh[h], NT), NEG_BIG)
                p = jnp.exp(s - lse[h : h + 1])
                ds = (p * (dot(v, doh[h], NT) - delta[h : h + 1])).astype(BF16)
                dv = dv + dot(p.astype(BF16), doh[h], NN)
                dk = dk + dot(ds, qh[h], NN)
                rows = slice(h * HDIM, (h + 1) * HDIM)
                dq_ref[rows] += dot(kt_ref[rows, pl.ds(at, TILE)], ds, NN)
            dk_ref[pl.ds(at, TILE), :] += dk
            dv_ref[pl.ds(at, TILE), :] += dv

        step(i, True)

        def body(j, _):
            step(j, False)
            return 0

        lax.fori_loop(info[1 + i], i, body, 0)
        out_ref[pl.ds(row, TILE), :width] = (dq_ref[...].T * HDIM**-0.5).astype(BF16)
        return 0

    lax.fori_loop(0, group_rows // TILE, q_block, 0)
    out_ref[:, width : 2 * width] = dk_ref[...].astype(BF16)
    out_ref[:, 2 * width :] = dv_ref[...].astype(BF16)


def attn_call(kernel, rows_own, info, operands, outs, scratch):
    smem = pl.BlockSpec(memory_space=pltpu.SMEM)
    vmem = pl.BlockSpec(memory_space=pltpu.VMEM)
    return pl.pallas_call(
        functools.partial(kernel, rows_own),
        out_shape=outs,
        in_specs=[smem] + [vmem] * len(operands),
        out_specs=[vmem] * len(outs),
        scratch_shapes=scratch,
        cost_estimate=pl.CostEstimate(
            flops=len(operands) * 6_000_000_000, transcendentals=0, bytes_accessed=8_000_000
        ),
    )(info, *operands)


def local(
    tokens,
    ln1_gain,
    ln1_bias,
    qkv_weight,
    out_weight,
    ln2_gain,
    ln2_bias,
    router_weight,
    up_weight,
    down_weight,
    expert_in,
    expert_out,
    mix,
    expert_ids,
    segment_ids,
    out_grad,
):
    slices = lax.axis_size(SLC)
    slc_index = lax.axis_index(SLC)
    exp_index = lax.axis_index(EXP)
    rows_own, features = tokens.shape
    group_rows = rows_own * slices
    experts = router_weight.shape[1]
    capacity = max(2, 2 * rows_own // experts)
    slots = experts * capacity
    width = qkv_weight.shape[2]
    heads = width // HDIM
    mix_dense = mix[0]
    mix_expert = mix[1]

    ids_own = lax.dynamic_slice_in_dim(expert_ids[:, 0], slc_index * rows_own, rows_own, 0)
    hot = (ids_own[:, None] == jnp.arange(experts, dtype=jnp.int32)[None]).astype(BF16)
    token_iota = jnp.arange(rows_own, dtype=jnp.int32)
    earlier = (token_iota[None] < token_iota[:, None]).astype(BF16)
    rank = jnp.sum(dot(earlier, hot, NN) * hot.astype(F32), -1).astype(jnp.int32)
    slot_own = ids_own * capacity + rank
    select = (jnp.arange(slots, dtype=jnp.int32)[:, None] == slot_own[None]).astype(BF16)

    def to_experts(rows):
        packed = dot(select, rows, NN, BF16).reshape(experts, capacity, features)
        return lax.all_to_all(packed, EXP, 0, 0, tiled=True).reshape(slots, features)

    def from_experts(rows):
        rows = rows.reshape(experts, capacity, features)
        return lax.all_to_all(rows, EXP, 0, 0, tiled=True).reshape(slots, features)

    x_own = tokens.astype(F32)
    xn1, hat_one, inv_one = norm_rows(x_own, ln1_gain, ln1_bias)
    xn1_low = xn1.astype(BF16)
    xg_one = jnp.concatenate(gather_rel(xn1_low, SLC), 0)
    qkv_flat = jnp.transpose(qkv_weight, (1, 0, 2)).reshape(features, 3 * width)
    qkv = dot(xg_one, qkv_flat, NN, BF16)
    seg = segment_ids[0]
    qstart = jnp.sum((seg[None] < seg[:, None]).astype(jnp.int32), -1)
    info = jnp.concatenate([slc_index[None].astype(jnp.int32), qstart[::TILE] // TILE])
    qstart = qstart[None]
    attn_o, lse = attn_call(
        attn_fwd_kernel,
        rows_own,
        info,
        (qkv, qstart),
        [
            jax.ShapeDtypeStruct((group_rows, width), BF16),
            jax.ShapeDtypeStruct((heads, group_rows), F32),
        ],
        [pltpu.VMEM((width, group_rows), BF16), pltpu.VMEM((width, TILE), F32)],
    )

    grad_slots = to_experts(after(out_grad, xn1_low))
    wo_all = jnp.concatenate(gather_rel(after(out_weight, xg_one), SLC), 0)
    grad_group = jnp.concatenate(gather_rel(after(out_grad, xg_one), SLC), 0)
    grad_hidden = lax.optimization_barrier(
        (mix_dense * dot(grad_group, down_weight, NT)).astype(BF16)
    )

    def blocks(value):
        return [value[r * rows_own : (r + 1) * rows_own] for r in range(slices)]

    o_own = jnp.concatenate(exchange_rel(blocks(attn_o), SLC), 1)
    attn_own = dot(o_own, wo_all, NN)
    h_own = x_own + attn_own
    xn2, hat_two, inv_two = norm_rows(h_own, ln2_gain, ln2_bias)
    xn2_low = xn2.astype(BF16)

    rows_in = to_experts(xn2_low)
    xg_two = jnp.concatenate(gather_rel(xn2_low, SLC), 0)
    win = gather_rel(after(expert_in[0], xn2_low), SLC)
    wout = gather_rel(after(expert_out[0], xn2_low), SLC)
    hidden, slope = gelu_pair(dot(xg_two, up_weight, NN, BF16))
    dense_part = dot(hidden, down_weight, NN, BF16)
    grad_up_pre = (grad_hidden.astype(F32) * slope.astype(F32)).astype(BF16)
    back_part = dot(grad_up_pre, up_weight, NT, BF16)
    grad_up = dot(xg_two, grad_up_pre, TN)
    grad_down_t = mix_dense * dot(grad_group, hidden, TN)
    rows_in = after(rows_in, dense_part, back_part, grad_up, grad_down_t)
    dense_back = scatter_rel(blocks(back_part), SLC)
    dense_own = scatter_rel(blocks(dense_part), SLC)
    sum_up, sum_down = scatter_rows([grad_up, grad_down_t], EXP)
    sum_down = sum_down.T

    prob_router = jax.nn.softmax(dot(rows_in, router_weight, NN), axis=-1)
    hot_here = (jnp.arange(experts, dtype=jnp.int32) == exp_index).astype(F32)[None]
    gate = jnp.sum(prob_router * hot_here, -1, keepdims=True)
    grad_rows = grad_slots.astype(F32)
    grad_eo = (mix_expert * gate * grad_rows).astype(BF16)
    slopes, act, ga = [], [], []
    eo = None
    for r in range(slices):
        z, slope = gelu_pair(dot(rows_in, win[r], NN, BF16))
        part = dot(z, wout[r], NN)
        eo = part if eo is None else eo + part
        slopes.append(slope)
        act.append(z)
    eo_low = eo.astype(BF16).astype(F32)
    gated = (gate * eo_low).astype(BF16)
    gated_home = from_experts(gated)
    row_dot = jnp.sum(grad_rows * eo_low, -1, keepdims=True)
    grad_gate = mix_expert * row_dot
    grad_logits = (gate * (hot_here - prob_router) * grad_gate).astype(BF16)
    back = dot(grad_logits, router_weight, NT)
    for r in range(slices):
        gz = dot(grad_eo, wout[r], NT)
        ga.append((gz * slopes[r].astype(F32)).astype(BF16))
        back = back + dot(ga[r], win[r], NT)
    back_low = back.astype(BF16)
    expert_back = dot(select, from_experts(back_low), TN)

    rows_late = after(rows_in, back_low)
    eo_late = after(grad_eo, back_low)
    grad_router = dot(rows_late, grad_logits, TN)
    gout = [dot(act[r], eo_late, TN) for r in range(slices)]
    gin = [dot(rows_late, ga[r], TN) for r in range(slices)]

    home, dense_tok, h_tok, grad_tok, _ = lax.optimization_barrier(
        (gated_home, dense_own, h_own, out_grad, back_low)
    )
    mixed_out = mix_dense * dense_tok + mix_expert * dot(select, home, TN)
    y_own = h_tok + mixed_out
    scalars = jnp.stack(
        [
            jnp.sum(h_tok * h_tok),
            jnp.sum(attn_own * attn_own),
            jnp.sum(mixed_out * mixed_out),
            jnp.sum(y_own * y_own),
            jnp.sum(grad_tok.astype(F32) * dense_tok),
            jnp.sum(gate * row_dot),
        ]
    )

    grad_xn2 = dense_back + expert_back
    grad_h_norm, grad_gain_two, grad_bias_two = norm_back(grad_xn2, hat_two, inv_two, ln2_gain)
    grad_h = out_grad.astype(F32) + grad_h_norm
    grad_attn = grad_h.astype(BF16)

    grad_o_own = dot(grad_attn, wo_all, NT, BF16)
    grad_o = jnp.concatenate(
        exchange_rel([grad_o_own[:, r * width : (r + 1) * width] for r in range(slices)], SLC),
        0,
    )
    (grad_qkv,) = attn_call(
        attn_bwd_kernel,
        rows_own,
        info,
        (qkv, qstart, attn_o, grad_o, lse),
        [jax.ShapeDtypeStruct((group_rows, 3 * width), BF16)],
        [
            pltpu.VMEM((width, group_rows), BF16),
            pltpu.VMEM((group_rows, width), F32),
            pltpu.VMEM((group_rows, width), F32),
            pltpu.VMEM((width, TILE), F32),
        ],
    )
    grad_xn1 = scatter_rel(blocks(dot(grad_qkv, qkv_flat, NT)), SLC)
    grad_qkv_w = dot(xg_one, grad_qkv, TN)
    grad_wo_t = dot(grad_attn, o_own, TN)
    grad_wo_t = scatter_rel([grad_wo_t[:, r * width : (r + 1) * width] for r in range(slices)], SLC)
    grad_x_norm, grad_gain_one, grad_bias_one = norm_back(grad_xn1, hat_one, inv_one, ln1_gain)
    grad_x = grad_h + grad_x_norm

    sum_qkv, sum_wo = scatter_rows([grad_qkv_w, grad_wo_t], EXP)
    sum_wo = sum_wo.T
    sum_qkv = jnp.transpose(sum_qkv.reshape(-1, 3, width), (1, 0, 2))

    small = jnp.concatenate(
        [
            grad_gain_one,
            grad_bias_one,
            grad_gain_two,
            grad_bias_two,
            grad_router.reshape(-1),
            jnp.pad(scalars, (0, features - scalars.shape[0])),
        ]
    ).reshape(-1, 128)
    small = sum_all(small, (EXP,))
    small = sum_all(small, (SLC,)).reshape(-1, features)

    def now(v):
        return v

    def then(v):
        return after(v, grad_o)

    grad_eout = scatter_rel(gout, SLC, (now, now, now, then))
    grad_ein = scatter_rel(gin, SLC, (then, then, now, now))
    scalars = small[4 + experts, :6]
    entry_total = group_rows * lax.axis_size(EXP) * features
    return (
        y_own,
        grad_x,
        small[0],
        small[1],
        sum_qkv,
        sum_wo,
        small[2],
        small[3],
        small[4 : 4 + experts].reshape(features, experts),
        sum_up,
        sum_down,
        grad_ein[None],
        grad_eout[None],
        scalars[4:6],
        jnp.sqrt(scalars[:4] / entry_total),
    )


def solution(mesh):
    in_specs = (
        P((EXP, SLC), None),
        P(),
        P(),
        P(None, None, SLC),
        P(SLC, None),
        P(),
        P(),
        P(),
        P(None, SLC),
        P(SLC, None),
        P(EXP, None, SLC),
        P(EXP, SLC, None),
        P(),
        P(EXP, None),
        P(EXP, None),
        P((EXP, SLC), None),
    )
    out_specs = (
        P((EXP, SLC), None),
        P((EXP, SLC), None),
        P(),
        P(),
        P(None, EXP, SLC),
        P(SLC, EXP),
        P(),
        P(),
        P(),
        P(EXP, SLC),
        P(SLC, EXP),
        P(EXP, None, SLC),
        P(EXP, SLC, None),
        P(),
        P(),
    )

    return jax.shard_map(local, mesh=mesh, in_specs=in_specs, out_specs=out_specs, check_vma=False)
```
